256 devices in a mesh: tgt: 32 (over y, x, z_lo), src: 8 (over z_hi, core).
Axes of the slice: x: 4, y: 4, z: 8 (z_hi: 4, z_lo: 2; z = z_hi * 2 + z_lo), core: 2. Of those that a mesh axis runs over, the one named last changes fastest.
Arguments:
- connectome: bfloat16 [4096, 51200], P('tgt', 'src'), may hold values from -0.02734375 to 0.02734375
- history: bfloat16 [32, 32, 51200], P('tgt', None, 'src'), may hold values from 0 to 5
- delays: int32 [32, 400], P('tgt', 'src'), may hold values from 16 to 32
- cycle_head: int32 [1], replicated, may hold values from 0 to 31
- outside_afferent: float32 [32], replicated, may hold values from 120 to 320
- init_state: float32 [6, 32, 4096], P(None, None, 'tgt'), may hold values from -4 to 4
- lead_field: bfloat16 [4096, 256], P('tgt'), may hold values from -0.09375 to 0.09375
Outputs:
- sensor_signal: float32 [32, 16, 256], P('tgt')
- final_state: float32 [6, 32, 4096], P(None, None, ('tgt', 'src'))
The draws below stay inside these ranges and needn't reach their ends.
Inputs may be any that keep to these rules, and one draw needn't show every extreme that they name: `cycle_head`: a slot of the history cycle.
All inputs are finite; a program needn't handle non-finite values.
Results may differ from the reference program's by a relative error of at most 0.003.
Values may be sent and summed in bfloat16 or wider, within the bound.
No kernel may reach another device: no remote copies, remote signals or barrier semaphores. Data moves between devices by JAX's collectives and lax.ppermute only.
A program may use at most 128 MiB of HBM per device.

```python
import math
import jax
import jax.numpy as jnp
from jax import lax

V = 51200
SENSORS = 256
MEM = 32
STEPS = 16
HIST = 32
SB = 128
TB = 128
TARGETS = 4096


def place_ends(result, own_key, smallest, high):
    index_at = [jax.random.randint(jax.random.fold_in(own_key, axis), (), 0, length) for axis, length in enumerate(result.shape)]
    widest = result.shape.index(max(result.shape))
    next_to = index_at[:widest] + [(index_at[widest] + 1) % result.shape[widest]] + index_at[widest + 1:]
    return result.at[tuple(index_at)].set(smallest).at[tuple(next_to)].set(high)


def levels(own_key, shape, split, smallest, top_value):
    gain = 1.0
    for axis_at, parts in split:
        heights = jax.random.uniform(jax.random.fold_in(jax.random.fold_in(own_key, 6), axis_at), (parts,), jnp.float32, smallest / len(split), top_value / len(split))
        gain = gain * jnp.repeat(jnp.exp(heights), shape[axis_at] // parts).reshape((-1,) + (1,) * (len(shape) - 1 - axis_at))
    return gain


def normal_values(stream_key, dims, spread, most, shards=(), kind=jnp.bfloat16):
    level = levels(stream_key, dims, shards, -0.22, 0.18) if shards else 1.0
    array = jax.random.normal(stream_key, dims, jnp.float32) * spread * level
    return jnp.minimum(jnp.maximum(array, -most), most).astype(kind)


def setup_inputs(seed: int = 0) -> dict:
    arg_keys = jax.random.split(jax.random.key(seed), 8)
    return {
        "connectome": normal_values(arg_keys[0], (TARGETS, V), V ** -0.5, 0.02734375, ((0, 32), (1, 8))),
        "history": jnp.clip(5.0 * jax.random.uniform(arg_keys[1], (HIST, MEM, V), jnp.float32) ** levels(arg_keys[1], (HIST, MEM, V), ((0, 32), (2, 8)), -0.2, 0.2), 0.0, 5.0).astype(jnp.bfloat16),
        "delays": place_ends(jax.random.randint(arg_keys[2], (TARGETS // TB, V // SB), STEPS, HIST + 1), jax.random.fold_in(arg_keys[2], 1), STEPS, HIST).astype(jnp.int32),
        "cycle_head": jax.random.randint(arg_keys[3], (1,), 0, HIST).astype(jnp.int32),
        "outside_afferent": jnp.clip(jnp.exp(jax.random.uniform(arg_keys[4], (MEM,), jnp.float32, math.log(120.0), math.log(320.0))), 120.0, 320.0),
        "init_state": normal_values(arg_keys[5], (6, MEM, TARGETS), 1.0, 4.0, ((2, 32),), jnp.float32),
        "lead_field": normal_values(arg_keys[6], (TARGETS, SENSORS), TARGETS ** -0.5, 0.09375, ((0, 32),)),
    }


integrator_step_width = 0.1
positive_synaptic_amplitude = 0.0325
negative_synaptic_amplitude = 0.11
interneuron_fraction = 0.5
global_link_scale = 30.0
stellate_contact_count = 135.0
recurrent_loop_contacts = 108.0
interneuron_contact_count = 33.75
peak_spike_rate = 5.0
logistic_slope_factor = 0.56
logistic_midpoint = 6.0


def spike_rate_response(cell_depolarization):
    return peak_spike_rate * jax.nn.sigmoid(logistic_slope_factor * (cell_depolarization - logistic_midpoint))


def advance(carry, applied_stimulus, outside_afferent):
    principal_cell_depolarization, stellate_mean_depolarization, interneuron_mean_depolarization, principal_cell_slope, excite_rate, interneuron_slope = carry
    next_principal_cell_slope = principal_cell_slope + integrator_step_width * (positive_synaptic_amplitude * spike_rate_response(stellate_mean_depolarization - interneuron_mean_depolarization) - 2.0 * principal_cell_slope - principal_cell_depolarization)
    summed_afferent_rate = outside_afferent[:, None] + recurrent_loop_contacts * spike_rate_response(stellate_contact_count * principal_cell_depolarization) + global_link_scale * applied_stimulus
    new_excite_rate = excite_rate + integrator_step_width * (positive_synaptic_amplitude * summed_afferent_rate - 2.0 * excite_rate - stellate_mean_depolarization)
    next_interneuron_slope = interneuron_slope + integrator_step_width * (negative_synaptic_amplitude * interneuron_contact_count * spike_rate_response(interneuron_contact_count * principal_cell_depolarization) - 2.0 * interneuron_fraction * interneuron_slope - interneuron_fraction * interneuron_fraction * interneuron_mean_depolarization)
    return (principal_cell_depolarization + integrator_step_width * principal_cell_slope, stellate_mean_depolarization + integrator_step_width * excite_rate, interneuron_mean_depolarization + integrator_step_width * interneuron_slope, next_principal_cell_slope, new_excite_rate, next_interneuron_slope)


def integrate(init_state, outside_afferent, coupling):
    def one_step(carry, applied_stimulus):
        fresh = advance(carry, applied_stimulus, outside_afferent)
        return fresh, fresh[1] - fresh[2]

    begin = tuple(init_state[member] for member in range(6))
    final, potentials = lax.scan(one_step, begin, coupling)
    return jnp.stack(final), potentials


def reference(connectome, history, delays, cycle_head, outside_afferent, init_state, lead_field):
    tiles = connectome.reshape(TARGETS // TB, TB, V // SB, SB)
    stacked = history.astype(jnp.float32).reshape(HIST, MEM, V // SB, SB)
    moments = jnp.arange(STEPS, dtype=jnp.int32)
    slot_ids = jnp.arange(HIST, dtype=jnp.int32)

    def one_block(pair):
        tile, lags = pair
        lag_slot = (cycle_head[0] + moments[:, None] - lags[None, :]) % HIST
        picker = (lag_slot[:, None, :] == slot_ids[None, :, None]).astype(jnp.float32)
        window = jnp.einsum("tkb,kmbs->tmbs", picker, stacked, precision=lax.Precision.HIGHEST)
        window = lax.optimization_barrier(window.astype(jnp.bfloat16)).astype(jnp.float32)
        return jnp.einsum("rbs,tmbs->tmr", tile.astype(jnp.float32), window, precision=lax.Precision.HIGHEST)

    blocks_out = lax.map(one_block, (tiles, delays))
    coupling = jnp.transpose(blocks_out, (1, 2, 0, 3)).reshape(STEPS, MEM, TARGETS)
    final_state, potentials = integrate(init_state, outside_afferent, coupling)
    potential = lax.optimization_barrier(potentials.astype(jnp.bfloat16)).astype(jnp.float32)
    signal = jnp.einsum("tmr,rs->mts", potential, lead_field.astype(jnp.float32), precision=lax.Precision.HIGHEST)
    return signal, final_state
```

```python
import jax
import jax.numpy as jnp
from jax import lax
from jax.experimental import pallas as pl
from jax.experimental.pallas import tpu as pltpu
from jax.sharding import Mesh, PartitionSpec as P

STEPS = 16
MEM = 32
SLOTS = 32
BLOCK = 128
HALF = 3200
BLOCKS = HALF // BLOCK
WIDE = HALF + 128
OFFSETS = (0, -1, 1, 2)
TGT = ("y", "x", "zl")
SRC = ("zh", "c")

step_width = 0.1
positive_amplitude = 0.0325
negative_amplitude = 0.11
interneuron_fraction = 0.5
link_scale = 30.0
stellate_contacts = 135.0
loop_contacts = 108.0
interneuron_contacts = 33.75
peak_rate = 5.0
slope_factor = 0.56
midpoint = 6.0


def up(v, axis):
    return lax.ppermute(v, axis, [(i, (i + 1) % 4) for i in range(4)])


def down(v, axis):
    return lax.ppermute(v, axis, [(i, (i + 3) % 4) for i in range(4)])


def swap(v, axis):
    return lax.ppermute(v, axis, [(0, 1), (1, 0)])


def ring_gather(piece, first, second):
    left, right = up(piece, first), down(piece, first)
    low, high = up(left[:, :16], first), down(right[:, 16:], first)
    row = jnp.concatenate([piece, left, right, jnp.concatenate([low, high], axis=1)], axis=0)
    row_left, row_right = up(row, second), down(row, second)
    far_low, far_high = up(row_left[:2], second), down(row_right[2:], second)
    return [row, row_left, row_right, far_low, far_high]


def coupling_kernel(slots, starts, place, *refs):
    pieces = refs[:10]
    tiles = refs[10:12]
    keep, send, lead, ordered, total = refs[12:]
    at = 0
    for ref in pieces:
        for i in range(ref.shape[0]):
            slot = slots[at]
            row = pl.multiple_of(slot * MEM, MEM)
            ordered[pl.ds(row, MEM), :] = ref[i, :, :HALF]

            @pl.when(slot < STEPS)
            def _():
                ordered[pl.ds(row + SLOTS * MEM, MEM), :] = ref[i, :, :HALF]

            tg = pl.multiple_of(slot * 16, 16)
            lead[pl.ds(tg, 16), :BLOCK] = ref[i, :16, HALF:]
            lead[pl.ds(tg, 16), BLOCK:] = ref[i, 16:, HALF:]
            at += 1
    zl = place[0]
    core = place[1]
    for h in range(2):

        def window(b):
            row = pl.multiple_of(starts[h, b] * MEM, MEM)
            return ordered[pl.ds(row, STEPS * MEM), b * BLOCK:(b + 1) * BLOCK]

        for b in range(0, BLOCKS, 2):
            if b + 1 < BLOCKS:
                rates = jnp.concatenate([window(b), window(b + 1)], axis=1)
                weights = tiles[h][:, b * BLOCK:(b + 2) * BLOCK]
            else:
                rates = window(b)
                weights = tiles[h][:, b * BLOCK:(b + 1) * BLOCK]
            part = lax.dot_general(
                weights, rates, (((1,), (1,)), ((), ())), preferred_element_type=jnp.float32
            )
            if b == 0:
                total[...] = part
            else:
                total[...] += part
        z = zl if h == 0 else 1 - zl
        for q in range(4):
            mine = pl.multiple_of(q * 32 + core * 16, 16)
            other = pl.multiple_of(q * 32 + (1 - core) * 16, 16)
            keep[pl.ds(z * 4 + q, 1)] = total[pl.ds(mine, 16), :][None]
            send[pl.ds(z * 4 + q, 1)] = total[pl.ds(other, 16), :][None]


def spike_rate(v):
    return peak_rate * jax.nn.sigmoid(slope_factor * (v - midpoint))


def integrate_kernel(parts, afferent, begin, final, potential, rows):
    coupling = parts[0]
    for i in range(1, 8):
        coupling = coupling + parts[i]
    outside = afferent[...]
    y0, y1, y2, y3, y4, y5 = (begin[i] for i in range(6))
    for t in range(STEPS):
        applied = coupling[:, t * MEM:(t + 1) * MEM]
        n3 = y3 + step_width * (positive_amplitude * spike_rate(y1 - y2) - 2.0 * y3 - y0)
        summed = outside + loop_contacts * spike_rate(stellate_contacts * y0) + link_scale * applied
        n4 = y4 + step_width * (positive_amplitude * summed - 2.0 * y4 - y1)
        n5 = y5 + step_width * (
            negative_amplitude * interneuron_contacts * spike_rate(interneuron_contacts * y0)
            - 2.0 * interneuron_fraction * y5
            - interneuron_fraction * interneuron_fraction * y2
        )
        y0, y1, y2 = y0 + step_width * y3, y1 + step_width * y4, y2 + step_width * y5
        y3, y4, y5 = n3, n4, n5
        rows[pl.ds(t, 16, stride=STEPS), :] = y1 - y2
    for i, v in enumerate((y0, y1, y2, y3, y4, y5)):
        final[i] = v
    potential[...] = rows[...].astype(jnp.bfloat16)


def vmem(n):
    return [pl.BlockSpec(memory_space=pltpu.VMEM)] * n


def smem(n):
    return [pl.BlockSpec(memory_space=pltpu.SMEM)] * n


def body(connectome, history, delays, cycle_head, outside_afferent, init_state, lead_field):
    y, x, zl = lax.axis_index("y"), lax.axis_index("x"), lax.axis_index("zl")
    zh, core = lax.axis_index("zh"), lax.axis_index("c")
    part = zh * 2 + core
    near, far = zl * HALF, (1 - zl) * HALF

    lead_rows = lax.dynamic_slice_in_dim(lead_field, part * 16, 16, 0)
    extra = jnp.concatenate([lead_rows[:, :128], lead_rows[:, 128:]], axis=0)[None]

    def cut(column):
        rates = lax.dynamic_slice_in_dim(history, column, HALF, 2)
        return jnp.concatenate([rates, extra], axis=2)

    own = cut(near)
    partner = swap(cut(far), "zl")
    start = (cycle_head[0] - delays) & (SLOTS - 1)
    start_own = lax.dynamic_slice_in_dim(start, zl * BLOCKS, BLOCKS, 1)
    start_other = swap(lax.dynamic_slice_in_dim(start, (1 - zl) * BLOCKS, BLOCKS, 1), "zl")
    tile_own = lax.dynamic_slice_in_dim(connectome, near, HALF, 1)
    tile_other = swap(lax.dynamic_slice_in_dim(connectome, far, HALF, 1), "zl")

    pieces = ring_gather(own, "x", "y") + ring_gather(partner, "y", "x")
    offsets = jnp.array(OFFSETS, jnp.int32)
    ys, xs = (y + offsets) & 3, (x + offsets) & 3
    slots = jnp.concatenate(
        [
            (ys[:, None] * 8 + xs[None, :] * 2 + zl).reshape(-1),
            (ys[None, :] * 8 + xs[:, None] * 2 + (1 - zl)).reshape(-1),
        ]
    )
    starts = jnp.concatenate([start_own, start_other], axis=0)
    place = jnp.stack([zl, core])

    keep, send, lead = pl.pallas_call(
        coupling_kernel,
        out_shape=(
            jax.ShapeDtypeStruct((8, 16, STEPS * MEM), jnp.float32),
            jax.ShapeDtypeStruct((8, 16, STEPS * MEM), jnp.float32),
            jax.ShapeDtypeStruct((SLOTS * 16, 256), jnp.bfloat16),
        ),
        in_specs=smem(3) + vmem(12),
        out_specs=tuple(vmem(3)),
        scratch_shapes=[
            pltpu.VMEM(((SLOTS + STEPS) * MEM, HALF), jnp.bfloat16),
            pltpu.VMEM((BLOCK, STEPS * MEM), jnp.float32),
        ],
        compiler_params=pltpu.CompilerParams(vmem_limit_bytes=40 << 20),
        name="coupling",
    )(slots, starts, place, *pieces, tile_own, tile_other)

    joined = keep + swap(send, "c")
    parts = lax.all_to_all(joined, ("zl", "zh"), 0, 0, tiled=True)

    begin = jnp.transpose(lax.dynamic_slice_in_dim(init_state, part * 16, 16, 2), (0, 2, 1))
    final, potential = pl.pallas_call(
        integrate_kernel,
        out_shape=(
            jax.ShapeDtypeStruct((6, 16, MEM), jnp.float32),
            jax.ShapeDtypeStruct((16 * STEPS, MEM), jnp.bfloat16),
        ),
        in_specs=vmem(3),
        out_specs=tuple(vmem(2)),
        scratch_shapes=[pltpu.VMEM((16 * STEPS, MEM), jnp.float32)],
        name="integrate",
    )(parts, outside_afferent[None, :], begin)
    final_state = jnp.transpose(final, (0, 2, 1))

    sent = potential.T
    got = lax.all_to_all(sent, TGT, 0, 0, tiled=True)
    signal = lax.dot_general(
        got.reshape(SLOTS * 16, STEPS), lead, (((0,), (0,)), ((), ())), preferred_element_type=jnp.float32
    )
    signal = signal + swap(signal, "c")
    ahead, behind = up(signal, "zh"), down(signal, "zh")
    across = lax.ppermute(signal, "zh", [(i, (i + 2) % 4) for i in range(4)])
    signal = (signal + across) + (ahead + behind)
    return signal[None], final_state


def solution(mesh):
    fine = Mesh(mesh.devices.reshape(4, 4, 2, 4, 2), TGT + SRC)
    in_specs = (
        P(TGT, SRC),
        P(TGT, None, SRC),
        P(TGT, SRC),
        P(),
        P(),
        P(None, None, TGT),
        P(TGT, None),
    )
    out_specs = (P(TGT, None, None), P(None, None, TGT + SRC))
    return jax.shard_map(body, mesh=fine, in_specs=in_specs, out_specs=out_specs, check_vma=False)
```

```python
import jax
import jax.numpy as jnp
from jax import lax
from jax.experimental import pallas as pl
from jax.experimental.pallas import tpu as pltpu
from jax.sharding import Mesh, PartitionSpec as P

STEPS = 16
MEM = 32
SLOTS = 32
BLOCK = 128
HALF = 3200
BLOCKS = HALF // BLOCK
SENSORS = 256
OFFSETS = (0, -1, 1, 2)
TGT = ("y", "x", "zl")
SRC = ("zh", "c")

step_width = 0.1
positive_amplitude = 0.0325
negative_amplitude = 0.11
interneuron_fraction = 0.5
link_scale = 30.0
stellate_contacts = 135.0
loop_contacts = 108.0
interneuron_contacts = 33.75
peak_rate = 5.0
slope_factor = 0.56
midpoint = 6.0


def up(v, axis):
    return lax.ppermute(v, axis, [(i, (i + 1) % 4) for i in range(4)])


def down(v, axis):
    return lax.ppermute(v, axis, [(i, (i + 3) % 4) for i in range(4)])


def swap(v, axis):
    return lax.ppermute(v, axis, [(0, 1), (1, 0)])


def ring_gather(piece, first, second):
    left, right = up(piece, first), down(piece, first)
    low, high = up(left[:, :16], first), down(right[:, 16:], first)
    row = jnp.concatenate([piece, left, right, jnp.concatenate([low, high], axis=1)], axis=0)
    row_left, row_right = up(row, second), down(row, second)
    far_low, far_high = up(row_left[:2], second), down(row_right[2:], second)
    return [row, row_left, row_right, far_low, far_high], left


def coupling_kernel(slots, starts, place, *refs):
    pieces = refs[:10]
    tiles = refs[10:12]
    keep, send, lead, ordered, total = refs[12:]
    at = 0
    for ref in pieces:
        for i in range(ref.shape[0]):
            slot = slots[at]
            row = pl.multiple_of(slot * MEM, MEM)
            ordered[pl.ds(row, MEM), :] = ref[i, :, :HALF]

            @pl.when(slot < STEPS)
            def _():
                ordered[pl.ds(row + SLOTS * MEM, MEM), :] = ref[i, :, :HALF]

            tg = pl.multiple_of(slot * 64, 64)
            lead[pl.ds(tg, MEM), :] = ref[i, :, HALF:HALF + SENSORS]
            lead[pl.ds(tg + MEM, MEM), :] = ref[i, :, HALF + SENSORS:]
            at += 1
    zl = place[0]
    core = place[1]
    for h in range(2):

        def window(b):
            row = pl.multiple_of(starts[h, b] * MEM, MEM)
            return ordered[pl.ds(row, STEPS * MEM), b * BLOCK:(b + 1) * BLOCK]

        for b in range(0, BLOCKS, 2):
            if b + 1 < BLOCKS:
                rates = jnp.concatenate([window(b), window(b + 1)], axis=1)
                weights = tiles[h][:, b * BLOCK:(b + 2) * BLOCK]
            else:
                rates = window(b)
                weights = tiles[h][:, b * BLOCK:(b + 1) * BLOCK]
            part = lax.dot_general(
                weights, rates, (((1,), (1,)), ((), ())), preferred_element_type=jnp.float32
            )
            if b == 0:
                total[...] = part
            else:
                total[...] += part
        z = zl if h == 0 else 1 - zl
        for q in range(4):
            mine = pl.multiple_of(q * 32 + core * 16, 16)
            other = pl.multiple_of(q * 32 + (1 - core) * 16, 16)
            keep[pl.ds(z * 4 + q, 1)] = total[pl.ds(mine, 16), :][None]
            send[pl.ds(z * 4 + q, 1)] = total[pl.ds(other, 16), :][None]


def spike_rate(v):
    return peak_rate * jax.nn.sigmoid(slope_factor * (v - midpoint))


def integrate_kernel(parts, afferent, begin, final, potential, rows):
    coupling = parts[0]
    for i in range(1, 8):
        coupling = coupling + parts[i]
    outside = afferent[...]
    y0, y1, y2, y3, y4, y5 = (begin[i].T for i in range(6))
    for t in range(STEPS):
        applied = coupling[:, t * MEM:(t + 1) * MEM]
        n3 = y3 + step_width * (positive_amplitude * spike_rate(y1 - y2) - 2.0 * y3 - y0)
        summed = outside + loop_contacts * spike_rate(stellate_contacts * y0) + link_scale * applied
        n4 = y4 + step_width * (positive_amplitude * summed - 2.0 * y4 - y1)
        n5 = y5 + step_width * (
            negative_amplitude * interneuron_contacts * spike_rate(interneuron_contacts * y0)
            - 2.0 * interneuron_fraction * y5
            - interneuron_fraction * interneuron_fraction * y2
        )
        y0, y1, y2 = y0 + step_width * y3, y1 + step_width * y4, y2 + step_width * y5
        y3, y4, y5 = n3, n4, n5
        rows[pl.ds(t, 16, stride=STEPS), :] = y1 - y2
    for i, v in enumerate((y0, y1, y2, y3, y4, y5)):
        final[i] = v.T
    flat = rows[...].T.astype(jnp.bfloat16)
    for i in range(4):
        potential[:, i, 0, :] = flat[:, :128]
        potential[:, i, 1, :] = flat[:, 128:]


def vmem(n):
    return [pl.BlockSpec(memory_space=pltpu.VMEM)] * n


def smem(n):
    return [pl.BlockSpec(memory_space=pltpu.SMEM)] * n


def body(connectome, history, delays, cycle_head, outside_afferent, init_state, lead_field):
    y, x, zl = lax.axis_index("y"), lax.axis_index("x"), lax.axis_index("zl")
    zh, core = lax.axis_index("zh"), lax.axis_index("c")
    part = zh * 2 + core
    near, far = zl * HALF, (1 - zl) * HALF

    lead_rows = lax.dynamic_index_in_dim(lead_field.reshape(4, 2, 16, SENSORS), core, 1, False)
    lead_rows = lead_rows.reshape(2, 32, SENSORS)
    extra = jnp.concatenate([lead_rows[0], lead_rows[1]], axis=1)[None]

    partner = swap(jnp.concatenate([lax.dynamic_slice_in_dim(history, far, HALF, 2), extra], axis=2), "zl")
    own = jnp.concatenate([lax.dynamic_slice_in_dim(history, near, HALF, 2), extra], axis=2)
    start = (cycle_head[0] - delays) & (SLOTS - 1)
    start_own = lax.dynamic_slice_in_dim(start, zl * BLOCKS, BLOCKS, 1)
    start_far = lax.dynamic_slice_in_dim(start, (1 - zl) * BLOCKS, BLOCKS, 1)
    tile_own = lax.dynamic_slice_in_dim(connectome, near, HALF, 1)
    tile_far = lax.dynamic_slice_in_dim(connectome, far, HALF, 1)
    note = jnp.pad(start_far.astype(jnp.bfloat16), ((0, 0), (0, BLOCK - BLOCKS)))
    tile_far = jnp.concatenate([tile_far, jnp.broadcast_to(note, (BLOCK, BLOCK))], axis=1)

    own_pieces, _ = ring_gather(own, "x", "y")
    other_pieces, early = ring_gather(partner, "y", "x")
    pieces = own_pieces + other_pieces
    tile_far, _ = lax.optimization_barrier((tile_far, early))
    tile_other = swap(tile_far, "zl")
    start_other = tile_other[:1, HALF:HALF + BLOCKS].astype(jnp.int32)
    offsets = jnp.array(OFFSETS, jnp.int32)
    ys, xs = (y + offsets) & 3, (x + offsets) & 3
    slots = jnp.concatenate(
        [
            (ys[:, None] * 8 + xs[None, :] * 2 + zl).reshape(-1),
            (ys[None, :] * 8 + xs[:, None] * 2 + (1 - zl)).reshape(-1),
        ]
    )
    starts = jnp.concatenate([start_own, start_other], axis=0)
    place = jnp.stack([zl, core])

    keep, send, lead = pl.pallas_call(
        coupling_kernel,
        out_shape=(
            jax.ShapeDtypeStruct((8, 16, STEPS * MEM), jnp.float32),
            jax.ShapeDtypeStruct((8, 16, STEPS * MEM), jnp.float32),
            jax.ShapeDtypeStruct((SLOTS * 64, SENSORS), jnp.bfloat16),
        ),
        in_specs=smem(3) + vmem(12),
        out_specs=tuple(vmem(3)),
        scratch_shapes=[
            pltpu.VMEM(((SLOTS + STEPS) * MEM, HALF), jnp.bfloat16),
            pltpu.VMEM((BLOCK, STEPS * MEM), jnp.float32),
        ],
        compiler_params=pltpu.CompilerParams(vmem_limit_bytes=24 << 20),
        name="coupling",
    )(slots, starts, place, *pieces, tile_own, tile_other)

    joined = keep + swap(send, "c")
    begin = lax.dynamic_slice_in_dim(init_state, part * 16, 16, 2)
    joined, begin, outside = lax.optimization_barrier((joined, begin, outside_afferent[None, :]))
    parts = lax.all_to_all(joined, ("zl", "zh"), 0, 0, tiled=True)
    final_state, potential = pl.pallas_call(
        integrate_kernel,
        out_shape=(
            jax.ShapeDtypeStruct((6, MEM, 16), jnp.float32),
            jax.ShapeDtypeStruct((MEM, 4, 2, 128), jnp.bfloat16),
        ),
        in_specs=vmem(3),
        out_specs=tuple(vmem(2)),
        scratch_shapes=[pltpu.VMEM((16 * STEPS, MEM), jnp.float32)],
        compiler_params=pltpu.CompilerParams(vmem_limit_bytes=4 << 20),
        name="integrate",
    )(parts, outside, begin)

    got = lax.all_to_all(potential.reshape(MEM * 4, 2, 128), TGT + ("zh",), 0, 0, tiled=True)
    signal = lax.dot_general(
        got.reshape(SLOTS * 64, STEPS), lead, (((0,), (0,)), ((), ())), preferred_element_type=jnp.float32
    )
    signal = signal + swap(signal, "c")
    return signal[None], final_state


def solution(mesh):
    fine = Mesh(mesh.devices.reshape(4, 4, 2, 4, 2), TGT + SRC)
    in_specs = (
        P(TGT, SRC),
        P(TGT, None, SRC),
        P(TGT, SRC),
        P(),
        P(),
        P(None, None, TGT),
        P(TGT, None),
    )
    out_specs = (P(TGT, None, None), P(None, None, TGT + SRC))
    return jax.shard_map(body, mesh=fine, in_specs=in_specs, out_specs=out_specs, check_vma=False)
```

```python
import jax
import jax.numpy as jnp
import numpy as np
from jax import lax
from jax.experimental import pallas as pl
from jax.experimental.pallas import tpu as pltpu
from jax.sharding import Mesh, PartitionSpec as P

STEPS = 16
MEM = 32
SLOTS = 32
BLOCK = 128
HALF = 3200
BLOCKS = HALF // BLOCK
SENSORS = 256
OFFSETS = (0, -1, 1, 2)
TGT = ("y", "x", "zl")
SRC = ("zh", "c")

step_width = 0.1
positive_amplitude = 0.0325
negative_amplitude = 0.11
interneuron_fraction = 0.5
link_scale = 30.0
stellate_contacts = 135.0
loop_contacts = 108.0
interneuron_contacts = 33.75
peak_rate = 5.0
slope_factor = 0.56
midpoint = 6.0


OUTER, INNER = np.repeat(OFFSETS, 4), np.tile(OFFSETS, 4)
PLACE_Y = np.concatenate([OUTER, INNER]).astype(np.int32)
PLACE_X = np.concatenate([INNER, OUTER]).astype(np.int32)
PLACE_Z = np.repeat(np.arange(2), 16).astype(np.int32)


def up(v, axis):
    return lax.ppermute(v, axis, [(i, (i + 1) % 4) for i in range(4)])


def down(v, axis):
    return lax.ppermute(v, axis, [(i, (i + 3) % 4) for i in range(4)])


def cut(v, at, size, axis):
    begin = [0] * v.ndim
    begin[axis] = at
    sizes = list(v.shape)
    sizes[axis] = size
    return lax.dynamic_slice(v, begin, sizes, allow_negative_indices=False)


def swap(v, axis):
    return lax.ppermute(v, axis, [(0, 1), (1, 0)])


def ring_gather(piece, first, second, mark=None):
    left, right = up(piece, first), down(piece, first)
    if mark is not None:
        left, right, _ = lax.optimization_barrier((left, right, mark))
    low, high = up(left[:, :16], first), down(right[:, 16:], first)
    row = jnp.concatenate([piece, left, right, jnp.concatenate([low, high], axis=1)], axis=0)
    row_left, row_right = up(row, second), down(row, second)
    far_low, far_high = up(row_left[:2], second), down(row_right[2:], second)
    return [row, row_left, row_right, far_low, far_high], left


def coupling_kernel(slots, starts, place, *refs):
    pieces = refs[:10]
    tiles = refs[10:12]
    keep, send, lead_out, ordered, total, lead, done = refs[12:]
    at = 0
    for ref in pieces:
        for i in range(ref.shape[0]):
            slot = slots[at]
            row = pl.multiple_of(slot * MEM, MEM)
            ordered[pl.ds(row, MEM), :] = ref[i, :, :HALF]

            @pl.when(slot < STEPS)
            def _():
                ordered[pl.ds(row + SLOTS * MEM, MEM), :] = ref[i, :, :HALF]

            tg = pl.multiple_of(slot * 64, 64)
            lead[pl.ds(tg, MEM), :] = ref[i, :, HALF:HALF + SENSORS]
            lead[pl.ds(tg + MEM, MEM), :] = ref[i, :, HALF + SENSORS:]
            at += 1
    store = pltpu.make_async_copy(lead, lead_out, done)
    store.start()
    zl = place[0]
    core = place[1]
    for h in range(2):

        def window(b):
            row = pl.multiple_of(starts[h, b] * MEM, MEM)
            return ordered[pl.ds(row, STEPS * MEM), b * BLOCK:(b + 1) * BLOCK]

        for b in range(0, BLOCKS, 2):
            if b + 1 < BLOCKS:
                rates = jnp.concatenate([window(b), window(b + 1)], axis=1)
                weights = tiles[h][:, b * BLOCK:(b + 2) * BLOCK]
            else:
                rates = window(b)
                weights = tiles[h][:, b * BLOCK:(b + 1) * BLOCK]
            part = lax.dot_general(
                weights, rates, (((1,), (1,)), ((), ())), preferred_element_type=jnp.float32
            )
            if b == 0:
                total[...] = part
            else:
                total[...] += part
        z = zl if h == 0 else 1 - zl
        for q in range(4):
            mine = pl.multiple_of(q * 32 + core * 16, 16)
            other = pl.multiple_of(q * 32 + (1 - core) * 16, 16)
            keep[pl.ds(z * 4 + q, 1)] = total[pl.ds(mine, 16), :][None]
            send[pl.ds(z * 4 + q, 1)] = total[pl.ds(other, 16), :][None]
    store.wait()


def spike_rate(v):
    return peak_rate * jax.nn.sigmoid(slope_factor * (v - midpoint))


def integrate_kernel(parts, afferent, begin, final, potential, rows):
    coupling = parts[0]
    for i in range(1, 8):
        coupling = coupling + parts[i]
    outside = afferent[...]
    y0, y1, y2, y3, y4, y5 = (begin[i].T for i in range(6))
    for t in range(STEPS):
        applied = coupling[:, t * MEM:(t + 1) * MEM]
        n3 = y3 + step_width * (positive_amplitude * spike_rate(y1 - y2) - 2.0 * y3 - y0)
        summed = outside + loop_contacts * spike_rate(stellate_contacts * y0) + link_scale * applied
        n4 = y4 + step_width * (positive_amplitude * summed - 2.0 * y4 - y1)
        n5 = y5 + step_width * (
            negative_amplitude * interneuron_contacts * spike_rate(interneuron_contacts * y0)
            - 2.0 * interneuron_fraction * y5
            - interneuron_fraction * interneuron_fraction * y2
        )
        y0, y1, y2 = y0 + step_width * y3, y1 + step_width * y4, y2 + step_width * y5
        y3, y4, y5 = n3, n4, n5
        rows[pl.ds(t, 16, stride=STEPS), :] = y1 - y2
    for i, v in enumerate((y0, y1, y2, y3, y4, y5)):
        final[i] = v
    flat = rows[...].T.astype(jnp.bfloat16)
    for i in range(4):
        potential[:, i, 0, :] = flat[:, :128]
        potential[:, i, 1, :] = flat[:, 128:]


def vmem(n):
    return [pl.BlockSpec(memory_space=pltpu.VMEM)] * n


def smem(n):
    return [pl.BlockSpec(memory_space=pltpu.SMEM)] * n


def body(connectome, history, delays, cycle_head, outside_afferent, init_state, lead_field):
    y, x, zl = lax.axis_index("y"), lax.axis_index("x"), lax.axis_index("zl")
    zh, core = lax.axis_index("zh"), lax.axis_index("c")
    near, far, part = zl * HALF, (1 - zl) * HALF, (zh * 2 + core) * 16
    near_block, far_block, other_zl = zl * BLOCKS, (1 - zl) * BLOCKS, 1 - zl
    (
        history, connectome, lead_field, delays, init_state,
        y, x, zl, core, near, far, part, near_block, far_block, other_zl,
    ) = lax.optimization_barrier(
        (
            history, connectome, lead_field, delays, init_state,
            y, x, zl, core, near, far, part, near_block, far_block, other_zl,
        )
    )

    lead_rows = cut(lead_field.reshape(4, 2, 16, SENSORS), core, 1, 1).reshape(2, 32, SENSORS)
    extra = jnp.concatenate([lead_rows[0], lead_rows[1]], axis=1)[None]
    sent = jnp.concatenate([cut(history, far, HALF, 2), extra], axis=2)
    history, sent = lax.optimization_barrier((history, sent))
    partner = swap(sent, "zl")
    own = jnp.concatenate([cut(history, near, HALF, 2), extra], axis=2)

    slots = ((y + PLACE_Y) & 3) * 8 + ((x + PLACE_X) & 3) * 2 + (zl ^ PLACE_Z)
    place = jnp.stack([zl, core])
    start = (cycle_head[0] - delays) & (SLOTS - 1)
    start_own = cut(start, near_block, BLOCKS, 1)
    start_far = cut(start, far_block, BLOCKS, 1)
    note = jnp.pad(start_far.astype(jnp.bfloat16), ((0, 0), (0, BLOCK - BLOCKS)))
    begin = cut(init_state, part, 16, 2)
    tile_own = cut(connectome, near, HALF, 1)
    tile_far = cut(connectome, far, HALF, 1)
    tile_far = jnp.concatenate([tile_far, jnp.broadcast_to(note, (BLOCK, BLOCK))], axis=1)

    own_pieces, _ = ring_gather(own, "x", "y", partner)
    other_pieces, early = ring_gather(partner, "y", "x")
    pieces = own_pieces + other_pieces
    tile_far, _ = lax.optimization_barrier((tile_far, early))
    tile_other = swap(tile_far, "zl")
    start_other = tile_other[:1, HALF:HALF + BLOCKS].astype(jnp.int32)
    starts = jnp.concatenate([start_own, start_other], axis=0)

    keep, send, lead = pl.pallas_call(
        coupling_kernel,
        out_shape=(
            jax.ShapeDtypeStruct((8, 16, STEPS * MEM), jnp.float32),
            jax.ShapeDtypeStruct((8, 16, STEPS * MEM), jnp.float32),
            jax.ShapeDtypeStruct((SLOTS * 64, SENSORS), jnp.bfloat16),
        ),
        in_specs=smem(3) + vmem(12),
        out_specs=(*vmem(2), pl.BlockSpec(memory_space=pl.ANY)),
        scratch_shapes=[
            pltpu.VMEM(((SLOTS + STEPS) * MEM, HALF), jnp.bfloat16),
            pltpu.VMEM((BLOCK, STEPS * MEM), jnp.float32),
            pltpu.VMEM((SLOTS * 64, SENSORS), jnp.bfloat16),
            pltpu.SemaphoreType.DMA,
        ],
        compiler_params=pltpu.CompilerParams(vmem_limit_bytes=24 << 20),
        name="coupling",
    )(slots, starts, place, *pieces, tile_own, tile_other)

    joined = keep + swap(send, "c")
    joined, begin, outside = lax.optimization_barrier((joined, begin, outside_afferent[None, :]))
    parts = lax.all_to_all(joined, ("zl", "zh"), 0, 0, tiled=True)
    final, potential = pl.pallas_call(
        integrate_kernel,
        out_shape=(
            jax.ShapeDtypeStruct((6, 16, MEM), jnp.float32),
            jax.ShapeDtypeStruct((MEM, 4, 2, 128), jnp.bfloat16),
        ),
        in_specs=vmem(3),
        out_specs=tuple(vmem(2)),
        scratch_shapes=[pltpu.VMEM((16 * STEPS, MEM), jnp.float32)],
        compiler_params=pltpu.CompilerParams(vmem_limit_bytes=4 << 20),
        name="integrate",
    )(parts, outside, begin)

    got = lax.all_to_all(potential.reshape(MEM * 4, 2, 128), TGT + ("zh",), 0, 0, tiled=True)
    signal = lax.dot_general(
        got.reshape(SLOTS * 64, STEPS), lead, (((0,), (0,)), ((), ())), preferred_element_type=jnp.float32
    )
    signal = signal + swap(signal, "c")
    return signal[None], jnp.transpose(final, (0, 2, 1))


def solution(mesh):
    fine = Mesh(mesh.devices.reshape(4, 4, 2, 4, 2), TGT + SRC)
    in_specs = (
        P(TGT, SRC),
        P(TGT, None, SRC),
        P(TGT, SRC),
        P(),
        P(),
        P(None, None, TGT),
        P(TGT, None),
    )
    out_specs = (P(TGT, None, None), P(None, None, TGT + SRC))
    return jax.shard_map(body, mesh=fine, in_specs=in_specs, out_specs=out_specs, check_vma=False)
```

```python
import jax
import jax.numpy as jnp
import numpy as np
from jax import lax
from jax.experimental import pallas as pl
from jax.experimental.pallas import tpu as pltpu
from jax.sharding import Mesh, PartitionSpec as P

STEPS = 16
MEM = 32
SLOTS = 32
BLOCK = 128
HALF = 3200
BLOCKS = HALF // BLOCK
SENSORS = 256
OFFSETS = (0, -1, 1, 2)
TGT = ("y", "x", "zl")
SRC = ("zh", "c")

step_width = 0.1
positive_amplitude = 0.0325
negative_amplitude = 0.11
interneuron_fraction = 0.5
link_scale = 30.0
stellate_contacts = 135.0
loop_contacts = 108.0
interneuron_contacts = 33.75
peak_rate = 5.0
slope_factor = 0.56
midpoint = 6.0


OUTER, INNER = np.repeat(OFFSETS, 4), np.tile(OFFSETS, 4)
PLACE_Y = np.concatenate([OUTER, INNER]).astype(np.int32)
PLACE_X = np.concatenate([INNER, OUTER]).astype(np.int32)
PLACE_Z = np.repeat(np.arange(2), 16).astype(np.int32)


def up(v, axis):
    return lax.ppermute(v, axis, [(i, (i + 1) % 4) for i in range(4)])


def down(v, axis):
    return lax.ppermute(v, axis, [(i, (i + 3) % 4) for i in range(4)])


def cut(v, at, size, axis):
    begin = [0] * v.ndim
    begin[axis] = at
    sizes = list(v.shape)
    sizes[axis] = size
    return lax.dynamic_slice(v, begin, sizes, allow_negative_indices=False)


def swap(v, axis):
    return lax.ppermute(v, axis, [(0, 1), (1, 0)])


def ring_gather(piece, first, second, mark=None):
    left, right = up(piece, first), down(piece, first)
    if mark is not None:
        left, right, _ = lax.optimization_barrier((left, right, mark))
    low, high = up(left[:, :16], first), down(right[:, 16:], first)
    row = jnp.concatenate([piece, left, right, jnp.concatenate([low, high], axis=1)], axis=0)
    row_left, row_right = up(row, second), down(row, second)
    far_low, far_high = up(row_left[:2], second), down(row_right[2:], second)
    return [row, row_left, row_right, far_low, far_high], left


def coupling_kernel(slots, starts, place, *refs):
    pieces = refs[:10]
    tiles = refs[10:12]
    keep, send, lead_out, ordered, total, wide, lead, done = refs[12:]
    at = 0
    for ref in pieces:
        for i in range(ref.shape[0]):
            slot = slots[at]
            row = pl.multiple_of(slot * MEM, MEM)
            ordered[pl.ds(row, MEM), :] = ref[i, :, :HALF]

            @pl.when(slot < STEPS)
            def _():
                ordered[pl.ds(row + SLOTS * MEM, MEM), :] = ref[i, :, :HALF]

            tg = pl.multiple_of(slot * 64, 64)
            lead[pl.ds(tg, MEM), :] = ref[i, :, HALF:HALF + SENSORS]
            lead[pl.ds(tg + MEM, MEM), :] = ref[i, :, HALF + SENSORS:]
            at += 1
    store = pltpu.make_async_copy(lead, lead_out, done)
    store.start()
    zl = place[0]
    core = place[1]
    for h in range(2):

        def window(b):
            row = pl.multiple_of(starts[h, b] * MEM, MEM)
            return ordered[pl.ds(row, STEPS * MEM), b * BLOCK:(b + 1) * BLOCK]

        for b in range(0, BLOCKS, 4):
            last = min(b + 4, BLOCKS)
            rates = jnp.concatenate([window(i) for i in range(b, last)], axis=1)
            weights = tiles[h][:, b * BLOCK:last * BLOCK]
            part = lax.dot_general(
                rates, weights, (((1,), (1,)), ((), ())), preferred_element_type=jnp.float32
            )
            if b == 0:
                wide[...] = part
            else:
                wide[...] += part
        total[...] = wide[...].T
        z = zl if h == 0 else 1 - zl
        for q in range(4):
            mine = pl.multiple_of(q * 32 + core * 16, 16)
            other = pl.multiple_of(q * 32 + (1 - core) * 16, 16)
            keep[pl.ds(z * 4 + q, 1)] = total[pl.ds(mine, 16), :][None]
            send[pl.ds(z * 4 + q, 1)] = total[pl.ds(other, 16), :][None]
    store.wait()


def spike_rate(v):
    return peak_rate * jax.nn.sigmoid(slope_factor * (v - midpoint))


def integrate_kernel(parts, afferent, begin, final, potential, rows):
    coupling = parts[0]
    for i in range(1, 8):
        coupling = coupling + parts[i]
    outside = afferent[...]
    y0, y1, y2, y3, y4, y5 = (begin[i].T for i in range(6))
    for t in range(STEPS):
        applied = coupling[:, t * MEM:(t + 1) * MEM]
        n3 = y3 + step_width * (positive_amplitude * spike_rate(y1 - y2) - 2.0 * y3 - y0)
        summed = outside + loop_contacts * spike_rate(stellate_contacts * y0) + link_scale * applied
        n4 = y4 + step_width * (positive_amplitude * summed - 2.0 * y4 - y1)
        n5 = y5 + step_width * (
            negative_amplitude * interneuron_contacts * spike_rate(interneuron_contacts * y0)
            - 2.0 * interneuron_fraction * y5
            - interneuron_fraction * interneuron_fraction * y2
        )
        y0, y1, y2 = y0 + step_width * y3, y1 + step_width * y4, y2 + step_width * y5
        y3, y4, y5 = n3, n4, n5
        rows[pl.ds(t, 16, stride=STEPS), :] = y1 - y2
    for i, v in enumerate((y0, y1, y2, y3, y4, y5)):
        final[i] = v.T
    flat = rows[...].T.astype(jnp.bfloat16)
    for i in range(4):
        potential[:, i, 0, :] = flat[:, :128]
        potential[:, i, 1, :] = flat[:, 128:]


def vmem(n):
    return [pl.BlockSpec(memory_space=pltpu.VMEM)] * n


def smem(n):
    return [pl.BlockSpec(memory_space=pltpu.SMEM)] * n


def body(connectome, history, delays, cycle_head, outside_afferent, init_state, lead_field):
    y, x, zl = lax.axis_index("y"), lax.axis_index("x"), lax.axis_index("zl")
    zh, core = lax.axis_index("zh"), lax.axis_index("c")
    near, far, part = zl * HALF, (1 - zl) * HALF, (zh * 2 + core) * 16
    near_block, far_block, other_zl = zl * BLOCKS, (1 - zl) * BLOCKS, 1 - zl
    (
        history, connectome, lead_field, delays, init_state,
        y, x, zl, core, near, far, part, near_block, far_block, other_zl,
    ) = lax.optimization_barrier(
        (
            history, connectome, lead_field, delays, init_state,
            y, x, zl, core, near, far, part, near_block, far_block, other_zl,
        )
    )

    lead_rows = cut(lead_field.reshape(4, 2, 16, SENSORS), core, 1, 1).reshape(2, 32, SENSORS)
    extra = jnp.concatenate([lead_rows[0], lead_rows[1]], axis=1)[None]
    sent = jnp.concatenate([cut(history, far, HALF, 2), extra], axis=2)
    history, sent = lax.optimization_barrier((history, sent))
    partner = swap(sent, "zl")
    own = jnp.concatenate([cut(history, near, HALF, 2), extra], axis=2)

    slots = ((y + PLACE_Y) & 3) * 8 + ((x + PLACE_X) & 3) * 2 + (zl ^ PLACE_Z)
    place = jnp.stack([zl, core])
    start = (cycle_head[0] - delays) & (SLOTS - 1)
    own, start = lax.optimization_barrier((own, start))
    start_own = cut(start, near_block, BLOCKS, 1)
    start_far = cut(start, far_block, BLOCKS, 1)
    note = jnp.pad(start_far.astype(jnp.bfloat16), ((0, 0), (0, BLOCK - BLOCKS)))
    begin = cut(init_state, part, 16, 2)
    tile_own = cut(connectome, near, HALF, 1)
    tile_far = cut(connectome, far, HALF, 1)
    tile_far = jnp.concatenate([tile_far, jnp.broadcast_to(note, (BLOCK, BLOCK))], axis=1)

    own_pieces, _ = ring_gather(own, "x", "y", partner)
    other_pieces, early = ring_gather(partner, "y", "x")
    pieces = own_pieces + other_pieces
    tile_far, _ = lax.optimization_barrier((tile_far, early))
    tile_other = swap(tile_far, "zl")
    start_other = tile_other[:1, HALF:HALF + BLOCKS].astype(jnp.int32)
    starts = jnp.concatenate([start_own, start_other], axis=0)

    keep, send, lead = pl.pallas_call(
        coupling_kernel,
        out_shape=(
            jax.ShapeDtypeStruct((8, 16, STEPS * MEM), jnp.float32),
            jax.ShapeDtypeStruct((8, 16, STEPS * MEM), jnp.float32),
            jax.ShapeDtypeStruct((SLOTS * 64, SENSORS), jnp.bfloat16),
        ),
        in_specs=smem(3) + vmem(12),
        out_specs=(*vmem(2), pl.BlockSpec(memory_space=pl.ANY)),
        scratch_shapes=[
            pltpu.VMEM(((SLOTS + STEPS) * MEM, HALF), jnp.bfloat16),
            pltpu.VMEM((BLOCK, STEPS * MEM), jnp.float32),
            pltpu.VMEM((STEPS * MEM, BLOCK), jnp.float32),
            pltpu.VMEM((SLOTS * 64, SENSORS), jnp.bfloat16),
            pltpu.SemaphoreType.DMA,
        ],
        compiler_params=pltpu.CompilerParams(vmem_limit_bytes=24 << 20),
        name="coupling",
    )(slots, starts, place, *pieces, tile_own, tile_other)

    joined = keep + swap(send, "c")
    joined, begin, outside = lax.optimization_barrier((joined, begin, outside_afferent[None, :]))
    parts = lax.all_to_all(joined, ("zl", "zh"), 0, 0, tiled=True)
    final, potential = pl.pallas_call(
        integrate_kernel,
        out_shape=(
            jax.ShapeDtypeStruct((6, MEM, 16), jnp.float32),
            jax.ShapeDtypeStruct((MEM, 4, 2, 128), jnp.bfloat16),
        ),
        in_specs=vmem(3),
        out_specs=tuple(vmem(2)),
        scratch_shapes=[pltpu.VMEM((16 * STEPS, MEM), jnp.float32)],
        compiler_params=pltpu.CompilerParams(vmem_limit_bytes=4 << 20),
        name="integrate",
    )(parts, outside, begin)

    got = lax.all_to_all(potential.reshape(MEM * 4, 2, 128), TGT + ("zh",), 0, 0, tiled=True)
    signal = lax.dot_general(
        got.reshape(SLOTS * 64, STEPS), lead, (((0,), (0,)), ((), ())), preferred_element_type=jnp.float32
    )
    signal = signal + swap(signal, "c")
    return signal[None], final


def solution(mesh):
    fine = Mesh(mesh.devices.reshape(4, 4, 2, 4, 2), TGT + SRC)
    in_specs = (
        P(TGT, SRC),
        P(TGT, None, SRC),
        P(TGT, SRC),
        P(),
        P(),
        P(None, None, TGT),
        P(TGT, None),
    )
    out_specs = (P(TGT, None, None), P(None, None, TGT + SRC))
    return jax.shard_map(body, mesh=fine, in_specs=in_specs, out_specs=out_specs, check_vma=False)
```

```python
import jax
import jax.numpy as jnp
import numpy as np
from jax import lax
from jax.experimental import pallas as pl
from jax.experimental.pallas import tpu as pltpu
from jax.sharding import Mesh, PartitionSpec as P

STEPS = 16
MEM = 32
SLOTS = 32
BLOCK = 128
HALF = 3200
BLOCKS = HALF // BLOCK
SENSORS = 256
OFFSETS = (0, -1, 1, 2)
TGT = ("y", "x", "zl")
SRC = ("zh", "c")

step_width = 0.1
positive_amplitude = 0.0325
negative_amplitude = 0.11
interneuron_fraction = 0.5
link_scale = 30.0
stellate_contacts = 135.0
loop_contacts = 108.0
interneuron_contacts = 33.75
peak_rate = 5.0
slope_factor = 0.56
midpoint = 6.0


OUTER, INNER = np.repeat(OFFSETS, 4), np.tile(OFFSETS, 4)
PLACE_Y = np.concatenate([INNER, OUTER]).astype(np.int32)
PLACE_X = np.concatenate([OUTER, INNER]).astype(np.int32)
PLACE_Z = np.repeat(np.arange(2), 16).astype(np.int32)


def up(v, axis):
    return lax.ppermute(v, axis, [(i, (i + 1) % 4) for i in range(4)])


def down(v, axis):
    return lax.ppermute(v, axis, [(i, (i + 3) % 4) for i in range(4)])


def cut(v, at, size, axis):
    begin = [0] * v.ndim
    begin[axis] = at
    sizes = list(v.shape)
    sizes[axis] = size
    return lax.dynamic_slice(v, begin, sizes, allow_negative_indices=False)


def swap(v, axis):
    return lax.ppermute(v, axis, [(0, 1), (1, 0)])


def ring_gather(piece, first, second, mark=None):
    left, right = up(piece, first), down(piece, first)
    if mark is not None:
        left, right, _ = lax.optimization_barrier((left, right, mark))
    low, high = up(left[:, :16], first), down(right[:, 16:], first)
    row = jnp.concatenate([piece, left, right, jnp.concatenate([low, high], axis=1)], axis=0)
    row_right = down(row, second)
    row_left = up(row, second)
    far_high = down(row_right[2:], second)
    far_low = up(row_left[:2], second)
    return [row, row_left, row_right, far_low, far_high], left


FIRST = (0, 1, 2, 3, 8, 9, 10, 11, 4, 5, 6, 7) + tuple(range(16, 28))
LAST = (14, 15, 12, 13) + tuple(range(28, 32))


def put(ref, i, slot, ordered, lead):
    row = pl.multiple_of(slot * MEM, MEM)
    ordered[pl.ds(row, MEM), :] = ref[i, :, :HALF]

    @pl.when(slot < STEPS)
    def _():
        ordered[pl.ds(row + SLOTS * MEM, MEM), :] = ref[i, :, :HALF]

    tg = pl.multiple_of(slot * 64, 64)
    lead[pl.ds(tg, MEM), :] = ref[i, :, HALF:HALF + SENSORS]
    lead[pl.ds(tg + MEM, MEM), :] = ref[i, :, HALF + SENSORS:]


def put_all(slots, order, pieces, ordered, lead):
    where = [(ref, i) for ref in pieces for i in range(ref.shape[0])]
    for at, (ref, i) in zip(order, where, strict=True):
        put(ref, i, slots[at], ordered, lead)


def place_kernel(slots, *refs):
    put_all(slots, FIRST, refs[:6], refs[6], refs[7])


def coupling_kernel(slots, starts, place, *refs):
    pieces = refs[:4]
    tiles = refs[4:6]
    _, _, keep, send, ordered, lead, lead_out, total, wide, done = refs[6:]
    put_all(slots, LAST, pieces, ordered, lead)
    store = pltpu.make_async_copy(lead, lead_out, done)
    store.start()
    zl = place[0]
    core = place[1]
    for h in range(2):

        def window(b):
            row = pl.multiple_of(starts[h, b] * MEM, MEM)
            return ordered[pl.ds(row, STEPS * MEM), b * BLOCK:(b + 1) * BLOCK]

        for b in range(0, BLOCKS, 4):
            last = min(b + 4, BLOCKS)
            rates = jnp.concatenate([window(i) for i in range(b, last)], axis=1)
            weights = tiles[h][:, b * BLOCK:last * BLOCK]
            part = lax.dot_general(
                rates, weights, (((1,), (1,)), ((), ())), preferred_element_type=jnp.float32
            )
            if b == 0:
                wide[...] = part
            else:
                wide[...] += part
        total[...] = wide[...].T
        z = zl if h == 0 else 1 - zl
        for q in range(4):
            mine = pl.multiple_of(q * 32 + core * 16, 16)
            other = pl.multiple_of(q * 32 + (1 - core) * 16, 16)
            keep[pl.ds(z * 4 + q, 1)] = total[pl.ds(mine, 16), :][None]
            send[pl.ds(z * 4 + q, 1)] = total[pl.ds(other, 16), :][None]
    store.wait()


def spike_rate(v):
    return peak_rate * jax.nn.sigmoid(slope_factor * (v - midpoint))


def integrate_kernel(parts, afferent, begin, final, potential, rows):
    coupling = parts[0]
    for i in range(1, 8):
        coupling = coupling + parts[i]
    outside = afferent[...]
    y0, y1, y2, y3, y4, y5 = (begin[i].T for i in range(6))
    for t in range(STEPS):
        applied = coupling[:, t * MEM:(t + 1) * MEM]
        n3 = y3 + step_width * (positive_amplitude * spike_rate(y1 - y2) - 2.0 * y3 - y0)
        summed = outside + loop_contacts * spike_rate(stellate_contacts * y0) + link_scale * applied
        n4 = y4 + step_width * (positive_amplitude * summed - 2.0 * y4 - y1)
        n5 = y5 + step_width * (
            negative_amplitude * interneuron_contacts * spike_rate(interneuron_contacts * y0)
            - 2.0 * interneuron_fraction * y5
            - interneuron_fraction * interneuron_fraction * y2
        )
        y0, y1, y2 = y0 + step_width * y3, y1 + step_width * y4, y2 + step_width * y5
        y3, y4, y5 = n3, n4, n5
        rows[pl.ds(t, 16, stride=STEPS), :] = y1 - y2
    for i, v in enumerate((y0, y1, y2, y3, y4, y5)):
        final[i] = v.T
    flat = rows[...].T.astype(jnp.bfloat16)
    for i in range(4):
        potential[:, i, 0, :] = flat[:, :128]
        potential[:, i, 1, :] = flat[:, 128:]


def vmem(n):
    return [pl.BlockSpec(memory_space=pltpu.VMEM)] * n


def smem(n):
    return [pl.BlockSpec(memory_space=pltpu.SMEM)] * n


def body(connectome, history, delays, cycle_head, outside_afferent, init_state, lead_field):
    y, x, zl = lax.axis_index("y"), lax.axis_index("x"), lax.axis_index("zl")
    zh, core = lax.axis_index("zh"), lax.axis_index("c")
    near, far, part = zl * HALF, (1 - zl) * HALF, (zh * 2 + core) * 16
    near_block, far_block, other_zl = zl * BLOCKS, (1 - zl) * BLOCKS, 1 - zl
    (
        history, connectome, lead_field, delays, init_state,
        y, x, zl, core, near, far, part, near_block, far_block, other_zl,
    ) = lax.optimization_barrier(
        (
            history, connectome, lead_field, delays, init_state,
            y, x, zl, core, near, far, part, near_block, far_block, other_zl,
        )
    )

    lead_rows = cut(lead_field.reshape(4, 2, 16, SENSORS), core, 1, 1).reshape(2, 32, SENSORS)
    extra = jnp.concatenate([lead_rows[0], lead_rows[1]], axis=1)[None]
    sent = jnp.concatenate([cut(history, far, HALF, 2), extra], axis=2)
    history, sent = lax.optimization_barrier((history, sent))
    partner = swap(sent, "zl")
    own = jnp.concatenate([cut(history, near, HALF, 2), extra], axis=2)

    slots = ((y + PLACE_Y) & 3) * 8 + ((x + PLACE_X) & 3) * 2 + (zl ^ PLACE_Z)
    place = jnp.stack([zl, core])
    start = (cycle_head[0] - delays) & (SLOTS - 1)
    own, start = lax.optimization_barrier((own, start))
    start_own = cut(start, near_block, BLOCKS, 1)
    start_far = cut(start, far_block, BLOCKS, 1)
    note = jnp.pad(start_far.astype(jnp.bfloat16), ((0, 0), (0, BLOCK - BLOCKS)))
    begin = cut(init_state, part, 16, 2)
    tile_own = cut(connectome, near, HALF, 1)
    tile_far = cut(connectome, far, HALF, 1)
    tile_far = jnp.concatenate([tile_far, jnp.broadcast_to(note, (BLOCK, BLOCK))], axis=1)

    own_pieces, _ = ring_gather(own, "y", "x", partner)
    other_pieces, early = ring_gather(partner, "x", "y")
    pieces = own_pieces + other_pieces
    tile_far, _ = lax.optimization_barrier((tile_far, early))
    tile_other = swap(tile_far, "zl")
    start_other = tile_other[:1, HALF:HALF + BLOCKS].astype(jnp.int32)
    starts = jnp.concatenate([start_own, start_other], axis=0)

    first = [own_pieces[0], own_pieces[2], own_pieces[1], *other_pieces[:3]]
    last = [own_pieces[4], own_pieces[3], *other_pieces[3:]]
    ordered, lead = pl.pallas_call(
        place_kernel,
        out_shape=(
            jax.ShapeDtypeStruct(((SLOTS + STEPS) * MEM, HALF), jnp.bfloat16),
            jax.ShapeDtypeStruct((SLOTS * 64, SENSORS), jnp.bfloat16),
        ),
        in_specs=smem(1) + vmem(6),
        out_specs=tuple(vmem(2)),
        compiler_params=pltpu.CompilerParams(vmem_limit_bytes=24 << 20),
        name="place",
    )(slots, *first)
    keep, send, ordered, lead, lead_out = pl.pallas_call(
        coupling_kernel,
        out_shape=(
            jax.ShapeDtypeStruct((8, 16, STEPS * MEM), jnp.float32),
            jax.ShapeDtypeStruct((8, 16, STEPS * MEM), jnp.float32),
            jax.ShapeDtypeStruct(((SLOTS + STEPS) * MEM, HALF), jnp.bfloat16),
            jax.ShapeDtypeStruct((SLOTS * 64, SENSORS), jnp.bfloat16),
            jax.ShapeDtypeStruct((SLOTS * 64, SENSORS), jnp.bfloat16),
        ),
        in_specs=smem(3) + vmem(8),
        out_specs=(*vmem(4), pl.BlockSpec(memory_space=pl.ANY)),
        scratch_shapes=[
            pltpu.VMEM((BLOCK, STEPS * MEM), jnp.float32),
            pltpu.VMEM((STEPS * MEM, BLOCK), jnp.float32),
            pltpu.SemaphoreType.DMA,
        ],
        input_output_aliases={9: 2, 10: 3},
        compiler_params=pltpu.CompilerParams(vmem_limit_bytes=24 << 20),
        name="coupling",
    )(slots, starts, place, *last, tile_own, tile_other, ordered, lead)
    lead = lead_out

    joined = keep + swap(send, "c")
    joined, begin, outside = lax.optimization_barrier((joined, begin, outside_afferent[None, :]))
    parts = lax.all_to_all(joined, ("zl", "zh"), 0, 0, tiled=True)
    final, potential = pl.pallas_call(
        integrate_kernel,
        out_shape=(
            jax.ShapeDtypeStruct((6, MEM, 16), jnp.float32),
            jax.ShapeDtypeStruct((MEM, 4, 2, 128), jnp.bfloat16),
        ),
        in_specs=vmem(3),
        out_specs=tuple(vmem(2)),
        scratch_shapes=[pltpu.VMEM((16 * STEPS, MEM), jnp.float32)],
        compiler_params=pltpu.CompilerParams(vmem_limit_bytes=4 << 20),
        name="integrate",
    )(parts, outside, begin)

    got = lax.all_to_all(potential.reshape(MEM * 4, 2, 128), TGT + ("zh",), 0, 0, tiled=True)
    signal = lax.dot_general(
        got.reshape(SLOTS * 64, STEPS), lead, (((0,), (0,)), ((), ())), preferred_element_type=jnp.float32
    )
    signal = signal + swap(signal, "c")
    return signal[None], final


def solution(mesh):
    fine = Mesh(mesh.devices.reshape(4, 4, 2, 4, 2), TGT + SRC)
    in_specs = (
        P(TGT, SRC),
        P(TGT, None, SRC),
        P(TGT, SRC),
        P(),
        P(),
        P(None, None, TGT),
        P(TGT, None),
    )
    out_specs = (P(TGT, None, None), P(None, None, TGT + SRC))
    return jax.shard_map(body, mesh=fine, in_specs=in_specs, out_specs=out_specs, check_vma=False)
```

```python
import jax
import jax.numpy as jnp
import numpy as np
from jax import lax
from jax.experimental import pallas as pl
from jax.experimental.pallas import tpu as pltpu
from jax.sharding import Mesh, PartitionSpec as P

STEPS = 16
MEM = 32
SLOTS = 32
BLOCK = 128
HALF = 3200
BLOCKS = HALF // BLOCK
SENSORS = 256
OFFSETS = (0, -1, 1, 2)
TGT = ("y", "x", "zl")
SRC = ("zh", "c")

step_width = 0.1
positive_amplitude = 0.0325
negative_amplitude = 0.11
interneuron_fraction = 0.5
link_scale = 30.0
stellate_contacts = 135.0
loop_contacts = 108.0
interneuron_contacts = 33.75
peak_rate = 5.0
slope_factor = 0.56
midpoint = 6.0


OUTER, INNER = np.repeat(OFFSETS, 4), np.tile(OFFSETS, 4)
PLACE_Y = np.concatenate([INNER, OUTER]).astype(np.int32)
PLACE_X = np.concatenate([OUTER, INNER]).astype(np.int32)
PLACE_Z = np.repeat(np.arange(2), 16).astype(np.int32)


def up(v, axis):
    return lax.ppermute(v, axis, [(i, (i + 1) % 4) for i in range(4)])


def down(v, axis):
    return lax.ppermute(v, axis, [(i, (i + 3) % 4) for i in range(4)])


def cut(v, at, size, axis):
    begin = [0] * v.ndim
    begin[axis] = at
    sizes = list(v.shape)
    sizes[axis] = size
    return lax.dynamic_slice(v, begin, sizes, allow_negative_indices=False)


def swap(v, axis):
    return lax.ppermute(v, axis, [(0, 1), (1, 0)])


def ring_gather(piece, first, second, mark=None):
    left, right = up(piece, first), down(piece, first)
    if mark is not None:
        left, right, _ = lax.optimization_barrier((left, right, mark))
    low, high = up(left[:, :16], first), down(right[:, 16:], first)
    row = jnp.concatenate([piece, left, right, jnp.concatenate([low, high], axis=1)], axis=0)
    row_right = down(row, second)
    row_left = up(row, second)
    far_high = down(row_right[2:], second)
    far_low = up(row_left[:2], second)
    return [row, row_left, row_right, far_low, far_high], left


FIRST = (0, 1, 2, 3, 8, 9, 10, 11, 4, 5, 6, 7) + tuple(range(16, 28))
LAST = (14, 15, 12, 13) + tuple(range(28, 32))


def put(ref, i, slot, ordered, lead):
    row = pl.multiple_of(slot * MEM, MEM)
    ordered[pl.ds(row, MEM), :] = ref[i, :, :HALF]

    @pl.when(slot < STEPS)
    def _():
        ordered[pl.ds(row + SLOTS * MEM, MEM), :] = ref[i, :, :HALF]

    tg = pl.multiple_of(slot * 64, 64)
    lead[pl.ds(tg, MEM), :] = ref[i, :, HALF:HALF + SENSORS]
    lead[pl.ds(tg + MEM, MEM), :] = ref[i, :, HALF + SENSORS:]


def put_all(slots, order, pieces, ordered, lead):
    where = [(ref, i) for ref in pieces for i in range(ref.shape[0])]
    for at, (ref, i) in zip(order, where, strict=True):
        put(ref, i, slots[at], ordered, lead)


def place_kernel(slots, *refs):
    put_all(slots, FIRST, refs[:6], refs[6], refs[7])


def coupling_kernel(slots, starts, place, *refs):
    pieces = refs[:4]
    tiles = refs[4:6]
    _, _, keep, send, ordered, lead, lead_out, total, wide, done = refs[6:]
    put_all(slots, LAST, pieces, ordered, lead)
    store = pltpu.make_async_copy(lead, lead_out, done)
    store.start()
    zl = place[0]
    core = place[1]
    for h in range(2):

        def window(b):
            row = pl.multiple_of(starts[h, b] * MEM, MEM)
            return ordered[pl.ds(row, STEPS * MEM), b * BLOCK:(b + 1) * BLOCK]

        for b in range(0, BLOCKS, 4):
            last = min(b + 4, BLOCKS)
            rates = jnp.concatenate([window(i) for i in range(b, last)], axis=1)
            weights = tiles[h][:, b * BLOCK:last * BLOCK]
            part = lax.dot_general(
                rates, weights, (((1,), (1,)), ((), ())), preferred_element_type=jnp.float32
            )
            if b == 0:
                wide[...] = part
            else:
                wide[...] += part
        total[...] = wide[...].T
        z = zl if h == 0 else 1 - zl
        for q in range(4):
            mine = pl.multiple_of(q * 32 + core * 16, 16)
            other = pl.multiple_of(q * 32 + (1 - core) * 16, 16)
            keep[pl.ds(z * 4 + q, 1)] = total[pl.ds(mine, 16), :][None]
            send[pl.ds(z * 4 + q, 1)] = total[pl.ds(other, 16), :][None]
    store.wait()


def spike_rate(v):
    return peak_rate * jax.nn.sigmoid(slope_factor * (v - midpoint))


def integrate_kernel(parts, afferent, begin, final, potential, rows):
    coupling = parts[0]
    for i in range(1, 8):
        coupling = coupling + parts[i]
    outside = afferent[...]
    y0, y1, y2, y3, y4, y5 = (begin[i].T for i in range(6))
    for t in range(STEPS):
        applied = coupling[:, t * MEM:(t + 1) * MEM]
        n3 = y3 + step_width * (positive_amplitude * spike_rate(y1 - y2) - 2.0 * y3 - y0)
        summed = outside + loop_contacts * spike_rate(stellate_contacts * y0) + link_scale * applied
        n4 = y4 + step_width * (positive_amplitude * summed - 2.0 * y4 - y1)
        n5 = y5 + step_width * (
            negative_amplitude * interneuron_contacts * spike_rate(interneuron_contacts * y0)
            - 2.0 * interneuron_fraction * y5
            - interneuron_fraction * interneuron_fraction * y2
        )
        y0, y1, y2 = y0 + step_width * y3, y1 + step_width * y4, y2 + step_width * y5
        y3, y4, y5 = n3, n4, n5
        rows[pl.ds(t, 16, stride=STEPS), :] = y1 - y2
    for i, v in enumerate((y0, y1, y2, y3, y4, y5)):
        final[i] = v.T
    flat = rows[...].T.astype(jnp.bfloat16)
    for i in range(4):
        potential[:, i, 0, :] = flat[:, :128]
        potential[:, i, 1, :] = flat[:, 128:]


def vmem(n):
    return [pl.BlockSpec(memory_space=pltpu.VMEM)] * n


def smem(n):
    return [pl.BlockSpec(memory_space=pltpu.SMEM)] * n


def body(connectome, history, delays, cycle_head, outside_afferent, init_state, lead_field):
    y, x, zl = lax.axis_index("y"), lax.axis_index("x"), lax.axis_index("zl")
    zh, core = lax.axis_index("zh"), lax.axis_index("c")
    near, far, part = zl * HALF, (1 - zl) * HALF, (zh * 2 + core) * 16
    near_block, far_block, other_zl = zl * BLOCKS, (1 - zl) * BLOCKS, 1 - zl
    (
        history, connectome, lead_field, delays, init_state,
        y, x, zl, core, near, far, part, near_block, far_block, other_zl,
    ) = lax.optimization_barrier(
        (
            history, connectome, lead_field, delays, init_state,
            y, x, zl, core, near, far, part, near_block, far_block, other_zl,
        )
    )

    lead_rows = cut(lead_field.reshape(4, 2, 16, SENSORS), core, 1, 1).reshape(2, 32, SENSORS)
    extra = jnp.concatenate([lead_rows[0], lead_rows[1]], axis=1)[None]
    sent = jnp.concatenate([cut(history, far, HALF, 2), extra], axis=2)
    history, sent = lax.optimization_barrier((history, sent))
    partner = swap(sent, "zl")
    own = jnp.concatenate([cut(history, near, HALF, 2), extra], axis=2)

    slots = ((y + PLACE_Y) & 3) * 8 + ((x + PLACE_X) & 3) * 2 + (zl ^ PLACE_Z)
    place = jnp.stack([zl, core])
    start = (cycle_head[0] - delays) & (SLOTS - 1)
    own, start = lax.optimization_barrier((own, start))
    start_own = cut(start, near_block, BLOCKS, 1)
    start_far = cut(start, far_block, BLOCKS, 1)
    note = jnp.pad(start_far.astype(jnp.bfloat16), ((0, 0), (0, BLOCK - BLOCKS)))
    begin = cut(init_state, part, 16, 2)
    tile_own = cut(connectome, near, HALF, 1)
    tile_far = cut(connectome, far, HALF, 1)
    tile_far = jnp.concatenate([tile_far, jnp.broadcast_to(note, (BLOCK, BLOCK))], axis=1)

    own_pieces, _ = ring_gather(own, "y", "x")
    other_pieces, early = ring_gather(partner, "x", "y")
    pieces = own_pieces + other_pieces
    tile_far, _ = lax.optimization_barrier((tile_far, early))
    tile_other = swap(tile_far, "zl")
    start_other = tile_other[:1, HALF:HALF + BLOCKS].astype(jnp.int32)
    starts = jnp.concatenate([start_own, start_other], axis=0)

    first = [own_pieces[0], own_pieces[2], own_pieces[1], *other_pieces[:3]]
    last = [own_pieces[4], own_pieces[3], *other_pieces[3:]]
    ordered, lead = pl.pallas_call(
        place_kernel,
        out_shape=(
            jax.ShapeDtypeStruct(((SLOTS + STEPS) * MEM, HALF), jnp.bfloat16),
            jax.ShapeDtypeStruct((SLOTS * 64, SENSORS), jnp.bfloat16),
        ),
        in_specs=smem(1) + vmem(6),
        out_specs=tuple(vmem(2)),
        compiler_params=pltpu.CompilerParams(vmem_limit_bytes=24 << 20),
        name="place",
    )(slots, *first)
    keep, send, ordered, lead, lead_out = pl.pallas_call(
        coupling_kernel,
        out_shape=(
            jax.ShapeDtypeStruct((8, 16, STEPS * MEM), jnp.float32),
            jax.ShapeDtypeStruct((8, 16, STEPS * MEM), jnp.float32),
            jax.ShapeDtypeStruct(((SLOTS + STEPS) * MEM, HALF), jnp.bfloat16),
            jax.ShapeDtypeStruct((SLOTS * 64, SENSORS), jnp.bfloat16),
            jax.ShapeDtypeStruct((SLOTS * 64, SENSORS), jnp.bfloat16),
        ),
        in_specs=smem(3) + vmem(8),
        out_specs=(*vmem(4), pl.BlockSpec(memory_space=pl.ANY)),
        scratch_shapes=[
            pltpu.VMEM((BLOCK, STEPS * MEM), jnp.float32),
            pltpu.VMEM((STEPS * MEM, BLOCK), jnp.float32),
            pltpu.SemaphoreType.DMA,
        ],
        input_output_aliases={9: 2, 10: 3},
        compiler_params=pltpu.CompilerParams(vmem_limit_bytes=24 << 20),
        name="coupling",
    )(slots, starts, place, *last, tile_own, tile_other, ordered, lead)
    lead = lead_out

    joined = keep + swap(send, "c")
    joined, begin, outside = lax.optimization_barrier((joined, begin, outside_afferent[None, :]))
    parts = lax.all_to_all(joined, ("zl", "zh"), 0, 0, tiled=True)
    final, potential = pl.pallas_call(
        integrate_kernel,
        out_shape=(
            jax.ShapeDtypeStruct((6, MEM, 16), jnp.float32),
            jax.ShapeDtypeStruct((MEM, 4, 2, 128), jnp.bfloat16),
        ),
        in_specs=vmem(3),
        out_specs=tuple(vmem(2)),
        scratch_shapes=[pltpu.VMEM((16 * STEPS, MEM), jnp.float32)],
        compiler_params=pltpu.CompilerParams(vmem_limit_bytes=4 << 20),
        name="integrate",
    )(parts, outside, begin)

    got = lax.all_to_all(potential.reshape(MEM * 4, 2, 128), TGT + ("zh",), 0, 0, tiled=True)
    signal = lax.dot_general(
        got.reshape(SLOTS * 64, STEPS), lead, (((0,), (0,)), ((), ())), preferred_element_type=jnp.float32
    )
    signal = signal + swap(signal, "c")
    return signal[None], final


def solution(mesh):
    fine = Mesh(mesh.devices.reshape(4, 4, 2, 4, 2), TGT + SRC)
    in_specs = (
        P(TGT, SRC),
        P(TGT, None, SRC),
        P(TGT, SRC),
        P(),
        P(),
        P(None, None, TGT),
        P(TGT, None),
    )
    out_specs = (P(TGT, None, None), P(None, None, TGT + SRC))
    return jax.shard_map(body, mesh=fine, in_specs=in_specs, out_specs=out_specs, check_vma=False)
```
